256 devices in a mesh: ent: 64 (over z, y, core), rel: 4 (over x).
Axes of the slice: x: 4, y: 4, z: 8, core: 2. Of those that a mesh axis runs over, the one named last changes fastest.
Arguments:
- entity_rows: bfloat16 [65536, 256], P('ent'), may hold values from -2.5 to 2.5
- request_rows: int32 [64, 64, 32], P('ent'), may hold values from 0 to 1023
- edge_heads: int32 [262144], P(('ent', 'rel')), may hold values from 0 to 1023
- edge_rels: int32 [262144], P(('ent', 'rel')), may hold values from 0 to 7
- edge_tails: int32 [262144], P(('ent', 'rel')), may hold values from 0 to 2047
- edge_counts: int32 [256], P(('ent', 'rel')), may hold values from 1 to 1024, 163840 in all
- negative_rows: int32 [65536], P(('ent', 'rel')), may hold values from 0 to 1023
- relation_blocks: bfloat16 [32, 8, 32, 32], P('rel'), may hold values from -1 to 1
Outputs:
- entity_grad: float32 [65536, 256], P('ent')
- relation_grad: float32 [32, 8, 32, 32], P('rel')
The draws below stay inside these ranges and needn't reach their ends.
Inputs may be any that keep to these rules, and one draw needn't show every extreme that they name: Edge slots of bucket b at or past edge_counts[b] are ignored; some bucket is full in every draw.
All inputs are finite; a program needn't handle non-finite values. No bound on the sum of `edge_counts` on one device may be relied on, other than what follows from the above.
Results may differ from the reference program's by a relative error of at most 0.009.
Values may be sent and summed in bfloat16 or wider, within the bound.
No kernel may reach another device: no remote copies, remote signals or barrier semaphores. Data moves between devices by JAX's collectives and lax.ppermute only.
A program may use at most 64 MiB of HBM per device.

```python
import math
import jax
import jax.numpy as jnp
import numpy as np
from jax import lax

D = 256
BLOCK = 32
R_DEV = 8
E_DEV = 1024
SLOTS = 32
EDGE_DEV = 1024
NEG = 256
PARTS_SIZE = 64
ENTITIES = 65536
RELATIONS = 32
BUCKETS = 256
EDGES = 262144
NEGS = 65536
N_ENT = 64
N_REL = 4


def touch_ends(entries, stream_key, low, top_value):
    shape = entries.shape
    index_at = [jax.random.randint(jax.random.fold_in(stream_key, axis), (), 0, shape[axis]) for axis in range(len(shape))]
    entries = entries.at[tuple(index_at)].set(low)
    longest = shape.index(max(shape))
    index_at[longest] = (index_at[longest] + 1) % shape[longest]
    return entries.at[tuple(index_at)].set(top_value)


def block_scale(key, dims, pieces, least, high):
    loudness = 1.0
    for dim, parts in pieces:
        steps = jax.random.uniform(jax.random.fold_in(jax.random.fold_in(key, 6), dim), (parts,), jnp.float32, least / len(pieces), high / len(pieces))
        loudness = loudness * jnp.repeat(jnp.exp(steps), dims[dim] // parts).reshape((-1,) + (1,) * (len(dims) - 1 - dim))
    return loudness


def split_up(count, total, reach, slope):
    portions = [(1 << 20) // math.isqrt(rank ** slope) + 1 for rank in range(2, count + 1)]
    surplus, holding = total - reach - (count - 1), [1] * (count - 1)
    while surplus > 0:
        candidates = [i for i in range(count - 1) if holding[i] < reach]
        pool, left = sum([portions[i] for i in candidates]), surplus
        for i in candidates:
            extra = min(reach - holding[i], max(1, left * portions[i] // pool), surplus)
            holding[i] = holding[i] + extra
            surplus = surplus - extra
    return np.array([reach] + holding)


def uneven_parts(rng, number_of, total, reach, skew):
    if number_of == 2:
        one = jax.random.randint(rng, (), max(1, total - reach), min(reach, total - 1) + 1)
        return jnp.stack([one, total - one])
    sizes = jnp.asarray(split_up(number_of, total, reach, skew), jnp.int32)
    couples = (number_of - 1) // 2
    source_of, taker = sizes[1:1 + 2 * couples:2], sizes[2:2 + 2 * couples:2]
    slack = jnp.minimum(source_of - 1, reach - taker)
    moved = jax.random.randint(jax.random.fold_in(rng, 1), (couples,), 0, 1 << 20) % (slack + 1)
    sizes = sizes.at[1:1 + 2 * couples:2].set(source_of - moved).at[2:2 + 2 * couples:2].set(taker + moved)
    return sizes[jax.random.permutation(jax.random.fold_in(rng, 2), number_of)]


def bell_draw(own_key, shape, scale, most, pieces=(), kind=jnp.bfloat16):
    result = scale * jax.random.normal(own_key, shape, jnp.float32)
    if pieces:
        result = result * block_scale(own_key, shape, pieces, -0.22, 0.18)
    return jnp.clip(result, -most, most).astype(kind)


def setup_inputs(seed: int = 0) -> dict:
    splits = jax.random.split(jax.random.key(seed), 9)
    entity_rows = bell_draw(splits[0], (ENTITIES, D), 0.35, 2.5, ((0, 64),))
    request_rows = touch_ends(jax.random.randint(splits[1], (PARTS_SIZE, PARTS_SIZE, SLOTS), 0, E_DEV), jax.random.fold_in(splits[1], 1), 0, E_DEV - 1).astype(jnp.int32)
    edge_heads = touch_ends(jax.random.randint(splits[2], (EDGES,), 0, E_DEV), jax.random.fold_in(splits[2], 1), 0, E_DEV - 1).astype(jnp.int32)
    edge_rels = touch_ends(jax.random.randint(splits[3], (EDGES,), 0, R_DEV), jax.random.fold_in(splits[3], 1), 0, R_DEV - 1).astype(jnp.int32)
    edge_tails = touch_ends(jax.random.randint(splits[4], (EDGES,), 0, PARTS_SIZE * SLOTS), jax.random.fold_in(splits[4], 1), 0, (PARTS_SIZE * SLOTS) - 1).astype(jnp.int32)
    edge_counts = uneven_parts(splits[5], BUCKETS, 5 * BUCKETS * EDGE_DEV // 8, EDGE_DEV, 2).astype(jnp.int32)
    negative_rows = touch_ends(jax.random.randint(splits[6], (NEGS,), 0, E_DEV), jax.random.fold_in(splits[6], 1), 0, E_DEV - 1).astype(jnp.int32)
    relation_blocks = bell_draw(splits[7], (RELATIONS, D // BLOCK, BLOCK, BLOCK), BLOCK ** -0.5, 1.0, ((0, 4),))
    return dict(entity_rows=entity_rows, request_rows=request_rows, edge_heads=edge_heads, edge_rels=edge_rels, edge_tails=edge_tails, edge_counts=edge_counts, negative_rows=negative_rows, relation_blocks=relation_blocks)


def reference(entity_rows, request_rows, edge_heads, edge_rels, edge_tails, edge_counts, negative_rows, relation_blocks):
    block_count = D // BLOCK
    grad_start = jnp.zeros((E_DEV * N_ENT, D), jnp.float32)
    rel_start = jnp.zeros((R_DEV * N_REL, block_count, BLOCK, BLOCK), jnp.float32)

    def bucket_step(running, bucket):
        entity_acc, relation_acc = running
        part_index = bucket // N_REL
        block_index = bucket % N_REL
        row_base = (part_index * E_DEV).astype(jnp.int32)
        source_table = lax.dynamic_slice_in_dim(entity_rows, row_base, E_DEV, 0)
        requests = lax.dynamic_index_in_dim(request_rows, part_index, 0, keepdims=False)
        rows_global = (jnp.arange(N_ENT, dtype=jnp.int32)[:, None] * E_DEV + requests).reshape(-1).astype(jnp.int32)
        fetched = entity_rows[rows_global]
        edge_base = (bucket * EDGE_DEV).astype(jnp.int32)
        head_ids = lax.dynamic_slice_in_dim(edge_heads, edge_base, EDGE_DEV, 0)
        rel_ids = lax.dynamic_slice_in_dim(edge_rels, edge_base, EDGE_DEV, 0)
        tail_ids = lax.dynamic_slice_in_dim(edge_tails, edge_base, EDGE_DEV, 0)
        neg_ids = lax.dynamic_slice_in_dim(negative_rows, (bucket * NEG).astype(jnp.int32), NEG, 0)
        live_count = edge_counts[bucket]
        live_mask = (jnp.arange(EDGE_DEV, dtype=jnp.int32) < live_count).astype(jnp.float32)
        operators = lax.dynamic_slice_in_dim(relation_blocks, (block_index * R_DEV).astype(jnp.int32), R_DEV, 0).astype(jnp.float32)
        head_rows = source_table[head_ids]
        tail_rows = fetched[tail_ids]
        neg_rows = source_table[neg_ids]
        rel_hot = (rel_ids[:, None] == jnp.arange(R_DEV, dtype=jnp.int32)[None, :]).astype(jnp.float32)
        head_split = head_rows.astype(jnp.float32).reshape(EDGE_DEV, block_count, BLOCK)
        proj_all = jnp.einsum('enb,rnbc->renc', head_split, operators)
        projected = jnp.sum(rel_hot.T[:, :, None, None] * proj_all, 0).reshape(EDGE_DEV, D).astype(jnp.bfloat16)
        projected_wide = projected.astype(jnp.float32)
        positive = jnp.sum(projected_wide * tail_rows.astype(jnp.float32), -1)
        negative = jnp.dot(projected, neg_rows.T, preferred_element_type=jnp.float32)
        pos_weight = -live_mask * jax.nn.sigmoid(-positive)
        neg_weight = (live_mask[:, None] * jax.nn.sigmoid(negative) / NEG).astype(jnp.bfloat16)
        grad_proj = (pos_weight[:, None] * tail_rows.astype(jnp.float32) + jnp.dot(neg_weight, neg_rows, preferred_element_type=jnp.float32)).astype(jnp.bfloat16)
        weighted = (pos_weight[:, None] * projected_wide).astype(jnp.bfloat16)
        neg_grad = jnp.dot(neg_weight.T, projected, preferred_element_type=jnp.float32).astype(jnp.bfloat16)
        grad_split = grad_proj.astype(jnp.float32).reshape(EDGE_DEV, block_count, BLOCK)
        back_all = jnp.einsum('enc,rnbc->renb', grad_split, operators)
        head_grad = jnp.sum(rel_hot.T[:, :, None, None] * back_all, 0).reshape(EDGE_DEV, D).astype(jnp.bfloat16)
        slot_grad = jax.ops.segment_sum(weighted.astype(jnp.float32), tail_ids, num_segments=N_ENT * SLOTS)
        entity_acc = entity_acc.at[row_base + head_ids].add(head_grad.astype(jnp.float32))
        entity_acc = entity_acc.at[row_base + neg_ids].add(neg_grad.astype(jnp.float32))
        entity_acc = entity_acc.at[rows_global].add(slot_grad)
        rel_term = jnp.einsum('er,enb,enc->rnbc', rel_hot, head_split, grad_split)
        rel_base = (block_index * R_DEV).astype(jnp.int32)
        current = lax.dynamic_slice_in_dim(relation_acc, rel_base, R_DEV, 0)
        relation_acc = lax.dynamic_update_slice_in_dim(relation_acc, current + rel_term, rel_base, 0)
        return (entity_acc, relation_acc), None

    buckets = jnp.arange(N_ENT * N_REL, dtype=jnp.int32)
    (entity_grad, relation_grad), _ = lax.scan(bucket_step, (grad_start, rel_start), buckets)
    return entity_grad, relation_grad
```

```python
import functools

import jax
import jax.numpy as jnp
from jax import lax
from jax.experimental import pallas as pl
from jax.experimental.pallas import tpu as pltpu
from jax.sharding import PartitionSpec as P

F32 = jnp.float32
BF16 = jnp.bfloat16
TILE = 256
SMEM = pl.BlockSpec(memory_space=pltpu.SMEM)
CONTRACT_LAST = (((1,), (1,)), ((), ()))


def iota(shape, axis):
    return lax.broadcasted_iota(jnp.int32, shape, axis)


def dot(a, b):
    return jnp.dot(a, b, preferred_element_type=F32)


def column(row):
    eye = iota((128, 128), 0) == iota((128, 128), 1)
    parts = []
    for k in range(row.shape[1] // 128):
        wide = jnp.broadcast_to(row[:, k * 128 : (k + 1) * 128].astype(F32), (128, 128))
        parts.append(jnp.sum(jnp.where(eye, wide, 0.0), axis=1, keepdims=True))
    return jnp.concatenate(parts, axis=0).astype(jnp.int32)


def hot_rows(col, width):
    return jnp.where(col == iota((col.shape[0], width), 1), 1.0, 0.0).astype(BF16)


def hot_columns(row, height):
    return jnp.where(row == iota((height, row.shape[1]), 0), 1.0, 0.0).astype(BF16)


def whole(shape):
    return pl.BlockSpec(shape, lambda *_: (0,) * len(shape))


def params(steps=1):
    return pltpu.CompilerParams(
        dimension_semantics=("arbitrary",) * (1 if steps else 0),
        vmem_limit_bytes=48 * 1024 * 1024,
    )


def cost(flops, nbytes):
    return pl.CostEstimate(flops=int(flops), bytes_accessed=int(nbytes), transcendentals=0)


def pick_kernel(share, scal, lists, table, out):
    n = lists.shape[0]
    wide = jnp.broadcast_to(lists[...].astype(F32)[:, None, :], (n, share, 128))
    wide = wide.reshape(n * share, 128)
    shape = (n * share, 128)
    wanted = iota(shape, 1) == scal[0] * share + iota(shape, 0) % share
    col = jnp.sum(jnp.where(wanted, wide, 0.0), axis=1, keepdims=True).astype(jnp.int32)
    out[...] = dot(hot_rows(col, table.shape[0]), table[...]).astype(BF16)


def rows_kernel(share, rels, scal, lists, out):
    n = lists.shape[0]
    wide = n * share
    ids = jnp.concatenate([lists[...], jnp.zeros((128 - n, 128), jnp.int32)], axis=0)
    turned = ids.astype(F32).T.astype(jnp.int32)
    spread = jnp.where(iota((128, wide), 1) // share == iota((128, wide), 0), 1.0, 0.0)
    spread = spread.astype(BF16)
    low = dot((turned & 31).astype(F32).astype(BF16), spread)
    high = dot((turned >> 5).astype(F32).astype(BF16), spread)
    value = high * 32.0 + low
    slot = iota((128, wide), 0)
    for c in range(rels):
        q = (scal[0] + c) % rels
        wanted = slot == q * share + iota((128, wide), 1) % share
        out[c : c + 1, :] = jnp.sum(jnp.where(wanted, value, 0.0), axis=0, keepdims=True).astype(
            jnp.int32
        )


def head_kernel(
    r_count, blocks, scal, heads, rels, negs, table, ops,
    proj_out, negpart_out, turned_out, nege_out, bd_out, neg_rows, neg_acc,
):
    step = pl.program_id(0)
    d = table.shape[1]
    width = d // blocks
    n_neg = neg_rows.shape[0]

    @pl.when(step == 0)
    def _():
        spread = jnp.where(iota((width, d), 1) % width == iota((width, d), 0), 1.0, 0.0)
        spread = spread.astype(BF16)
        inside = iota((d, d), 0) // width == iota((d, d), 1) // width
        for r in range(r_count):
            full = dot(ops[r * d : (r + 1) * d, :], spread)
            bd_out[r * d : (r + 1) * d, :] = jnp.where(inside, full, 0.0).astype(BF16)
        neg_hot = hot_rows(column(negs[...]), table.shape[0])
        neg_rows[...] = dot(neg_hot, table[...]).astype(BF16)
        neg_acc[...] = jnp.zeros_like(neg_acc)

    head_wide = dot(hot_rows(column(heads[0]), table.shape[0]), table[...])
    head = head_wide.astype(BF16)
    turned_out[...] = head_wide.T.astype(BF16)
    rel_col = column(rels[0])
    proj = jnp.zeros((TILE, d), F32)
    for r in range(r_count):
        masked = jnp.where(rel_col == r, head_wide, 0.0).astype(BF16)
        proj = proj + dot(masked, bd_out[r * d : (r + 1) * d, :])
    proj = proj.astype(BF16)
    proj_out[...] = proj
    negative = lax.dot_general(proj, neg_rows[...], CONTRACT_LAST, preferred_element_type=F32)
    live = step * TILE + iota((TILE, n_neg), 0) < scal[1]
    weight = jnp.where(live, jax.nn.sigmoid(negative) / n_neg, 0.0)
    negpart_out[...] = dot(weight.astype(BF16), neg_rows[...])
    neg_acc[...] += dot(weight.T.astype(BF16), proj)

    @pl.when(step == pl.num_programs(0) - 1)
    def _():
        grads = neg_acc[...].astype(BF16)
        for k in range(table.shape[0] // TILE):
            hot = hot_columns(negs[...] - k * TILE, TILE)
            nege_out[k * TILE : (k + 1) * TILE, :] = dot(hot, grads)


def tail_kernel(n_rel, share, scal, tails, proj, negpart, *refs):
    chunks, (gp_out, *outs), (weighted, places) = (
        refs[:n_rel], refs[n_rel : 2 * n_rel + 1], refs[2 * n_rel + 1 :],
    )
    step = pl.program_id(0)
    edges = pl.num_programs(0) * TILE
    rows = chunks[0].shape[0]
    slots = share * n_rel
    t = tails[0]
    slot = t % slots
    place = (slot // share - scal[0] + n_rel) % n_rel * rows
    place = place + t // slots * share + slot % share
    places[:, pl.ds(pl.multiple_of(step * TILE, TILE), TILE)] = place
    col = column(place)
    tail = jnp.zeros((TILE, proj.shape[1]), F32)
    for c in range(n_rel):
        tail = tail + dot(hot_rows(col - c * rows, rows), chunks[c][...])
    wide = proj[...].astype(F32)
    positive = jnp.sum(wide * tail, axis=1, keepdims=True)
    live = step * TILE + iota((TILE, 1), 0) < scal[1]
    pos_weight = jnp.where(live, -jax.nn.sigmoid(-positive), 0.0)
    gp_out[...] = (pos_weight * tail + negpart[...]).astype(BF16)
    weighted[pl.ds(pl.multiple_of(step * TILE, TILE), TILE), :] = (pos_weight * wide).astype(BF16)

    @pl.when(step == pl.num_programs(0) - 1)
    def _():
        for c in range(n_rel):
            for k in range(rows // TILE):
                hot = hot_columns(places[...] - (c * rows + k * TILE), TILE)
                outs[c][k * TILE : (k + 1) * TILE, :] = dot(hot, weighted[...]).astype(BF16)


def grad_kernel(
    blocks, n_rel, scal, heads, rels, gp, turned, nege, bd,
    rel_out, *refs,
):
    outs, (head_acc, rows_acc) = refs[:n_rel], refs[n_rel:]
    step = pl.program_id(0)
    edges, d = gp.shape
    width = d // blocks
    rel_row = rels[...]
    grads = gp[...]

    @pl.when(step == 0)
    def _():
        head_acc[...] = jnp.zeros_like(head_acc)

    masked = jnp.where(rel_row == step, turned[...].astype(F32), 0.0).astype(BF16)
    outer = dot(masked, grads)
    inside = iota((d, d), 0) // width == iota((d, d), 1) // width
    outer = jnp.where(inside, outer, 0.0)
    packed = outer[:width]
    for n in range(1, blocks):
        packed = packed + outer[n * width : (n + 1) * width]
    for half in range(d // 128):
        start = pl.multiple_of((half * pl.num_programs(0) + step) * width, width)
        rel_out[pl.ds(start, width), :] = packed[:, half * 128 : (half + 1) * 128].astype(BF16)
    for k in range(edges // TILE):
        part = pl.ds(k * TILE, TILE)
        rel_col = column(rel_row[:, k * TILE : (k + 1) * TILE])
        mine = jnp.where(rel_col == step, gp[part, :].astype(F32), 0.0).astype(BF16)
        head_acc[part, :] += lax.dot_general(mine, bd[...], CONTRACT_LAST, preferred_element_type=F32)

    @pl.when(step == pl.num_programs(0) - 1)
    def _():
        rows = nege.shape[0] // n_rel
        head_grad = head_acc[...].astype(BF16)
        for k in range(nege.shape[0] // TILE):
            part = slice(k * TILE, (k + 1) * TILE)
            rows_acc[part, :] = nege[part, :] + dot(hot_columns(heads[...] - k * TILE, TILE), head_grad)
        for c in range(n_rel):
            start = pl.multiple_of((scal[0] + c) % n_rel * rows, rows)
            outs[c][...] = rows_acc[pl.ds(start, rows), :].astype(BF16)


def owner_kernel(n_rel, scal, ids, *refs):
    slots, terms, out = refs[:n_rel], refs[n_rel : 2 * n_rel], refs[2 * n_rel]
    step = pl.program_id(0)
    rows = out.shape[0]
    total = jnp.zeros(out.shape, F32)
    for c in range(n_rel):
        total = total + dot(hot_columns(ids[c : c + 1, :] - step * rows, rows), slots[c][...])
    for c in range(n_rel):
        @pl.when((scal[0] + c) % n_rel == step)
        def _(c=c):
            out[...] = total + terms[c][...].astype(F32)


def relation_kernel(r_count, blocks, width, x, out):
    per = 128 // width
    for r in range(r_count):
        for n in range(blocks):
            start = (n // per * r_count + r) * width
            block = x[start : start + width, n % per * width : (n % per + 1) * width]
            out[r, n] = block.astype(F32)


def ring(x, n_rel, shift):
    return lax.ppermute(x, "rel", [((k + shift) % n_rel, k) for k in range(n_rel)])


def local(
    entity_rows, request_rows, edge_heads, edge_rels, edge_tails, edge_counts, negative_rows,
    relation_blocks,
):
    rows, d = entity_rows.shape
    parts, slots = request_rows.shape[1:]
    r_count, blocks, width = relation_blocks.shape[:3]
    edges, n_neg = edge_heads.shape[0], negative_rows.shape[0]
    n_rel = lax.axis_size("rel")
    share = slots // n_rel
    held = parts * share
    steps = edges // TILE
    me = lax.axis_index("rel").astype(jnp.int32)
    scal = jnp.concatenate([me.reshape(1), edge_counts])
    shaped = jax.ShapeDtypeStruct

    wide_lists = jnp.pad(request_rows.reshape(parts, slots), ((0, 0), (0, 128 - slots)))
    lists = lax.all_to_all(wide_lists, "ent", 0, 0, tiled=True)

    heads = edge_heads.reshape(steps, 1, TILE)
    rels = edge_rels.reshape(steps, 1, TILE)
    tails = edge_tails.reshape(steps, 1, TILE)
    negs = negative_rows.reshape(1, n_neg)
    id_block = pl.BlockSpec((1, 1, TILE), lambda i: (i, 0, 0))
    edge_block = pl.BlockSpec((TILE, d), lambda i: (i, 0))

    proj, negpart, turned, nege, bd = pl.pallas_call(
        functools.partial(head_kernel, r_count, blocks),
        grid=(steps,),
        in_specs=[
            SMEM, id_block, id_block, whole((1, n_neg)), whole((rows, d)),
            whole((r_count * d, width)),
        ],
        out_specs=[
            edge_block, edge_block, pl.BlockSpec((d, TILE), lambda i: (0, i)), whole((rows, d)),
            whole((r_count * d, d)),
        ],
        out_shape=[
            shaped((edges, d), BF16), shaped((edges, d), F32), shaped((d, edges), BF16),
            shaped((rows, d), F32), shaped((r_count * d, d), BF16),
        ],
        scratch_shapes=[pltpu.VMEM((n_neg, d), BF16), pltpu.VMEM((n_neg, d), F32)],
        compiler_params=params(),
        cost_estimate=cost(3e9, 6e6),
        name="head_step",
    )(scal, heads, rels, negs, entity_rows, relation_blocks.reshape(r_count * d, width))

    picked = pl.pallas_call(
        functools.partial(pick_kernel, share),
        in_specs=[SMEM, whole((parts, 128)), whole((rows, d))],
        out_specs=whole((held, d)),
        out_shape=shaped((held, d), BF16),
        compiler_params=params(0),
        cost_estimate=cost(2 * held * rows * d, 1e6),
        name="pick",
    )(scal, lists, entity_rows)
    list_rows = pl.pallas_call(
        functools.partial(rows_kernel, share, n_rel),
        in_specs=[SMEM, whole((parts, 128))],
        out_specs=whole((n_rel, held)),
        out_shape=shaped((n_rel, held), jnp.int32),
        compiler_params=params(0),
        cost_estimate=cost(1e8, 1e5),
        name="list_rows",
    )(scal, lists)

    fetched = [lax.all_to_all(picked, "ent", 0, 0, tiled=True)]
    fetched += [ring(fetched[0], n_rel, c) for c in range(1, n_rel)]

    grad_proj, *slot_parts = pl.pallas_call(
        functools.partial(tail_kernel, n_rel, share),
        grid=(steps,),
        in_specs=[SMEM, id_block, edge_block, edge_block] + [whole((held, d))] * n_rel,
        out_specs=[edge_block] + [whole((held, d))] * n_rel,
        out_shape=[shaped((edges, d), BF16)] + [shaped((held, d), BF16)] * n_rel,
        scratch_shapes=[pltpu.VMEM((edges, d), BF16), pltpu.VMEM((1, edges), jnp.int32)],
        compiler_params=params(),
        cost_estimate=cost(3e9, 5e6),
        name="tail_step",
    )(scal, tails, proj, negpart, *fetched)
    slot_sum = slot_parts[0].astype(F32)
    for c in range(1, n_rel):
        slot_sum = slot_sum + ring(slot_parts[c], n_rel, n_rel - c).astype(F32)

    rel_part, *row_parts = pl.pallas_call(
        functools.partial(grad_kernel, blocks, n_rel),
        grid=(r_count,),
        in_specs=[
            SMEM, whole((1, edges)), whole((1, edges)), whole((edges, d)), whole((d, edges)),
            whole((rows, d)), pl.BlockSpec((d, d), lambda r: (r, 0)),
        ],
        out_specs=[whole((r_count * width * d // 128, 128))] + [whole((rows // n_rel, d))] * n_rel,
        out_shape=[shaped((r_count * width * d // 128, 128), BF16)]
        + [shaped((rows // n_rel, d), BF16)] * n_rel,
        scratch_shapes=[pltpu.VMEM((edges, d), F32), pltpu.VMEM((rows, d), F32)],
        compiler_params=params(),
        cost_estimate=cost(3e9, 6e6),
        name="grad_step",
    )(scal, edge_heads.reshape(1, edges), edge_rels.reshape(1, edges), grad_proj, turned, nege, bd)

    packed = jnp.concatenate([slot_sum.astype(BF16), rel_part], axis=1)
    returned = lax.all_to_all(packed, "ent", 0, 0, tiled=True)
    slot_back = [returned[:, :d]]
    slot_back += [ring(slot_back[0], n_rel, c) for c in range(1, n_rel)]
    rel_sum = jnp.sum(returned[:, d:].reshape(parts, -1, 128).astype(F32), 0).astype(BF16)
    rel_all = jnp.broadcast_to(rel_sum[None], (parts,) + rel_sum.shape).reshape(-1, 128)
    rel_all = lax.all_to_all(rel_all, "ent", 0, 0, tiled=True)

    row_sum = row_parts[0].astype(F32)
    for c in range(1, n_rel):
        row_sum = row_sum + ring(row_parts[c], n_rel, n_rel - c).astype(F32)
    row_terms = [row_sum.astype(BF16)]
    row_terms += [ring(row_terms[0], n_rel, c) for c in range(1, n_rel)]

    entity_grad = pl.pallas_call(
        functools.partial(owner_kernel, n_rel),
        grid=(n_rel,),
        in_specs=[SMEM, whole((n_rel, held))]
        + [whole((held, d))] * n_rel
        + [whole((rows // n_rel, d))] * n_rel,
        out_specs=pl.BlockSpec((rows // n_rel, d), lambda q: (q, 0)),
        out_shape=shaped((rows, d), F32),
        compiler_params=params(),
        cost_estimate=cost(1e9, 3e6),
        name="owner_add",
    )(scal, list_rows, *slot_back, *row_terms)
    relation_grad = pl.pallas_call(
        functools.partial(relation_kernel, r_count, blocks, width),
        in_specs=[whole(rel_all.shape)],
        out_specs=whole(relation_blocks.shape),
        out_shape=shaped(relation_blocks.shape, F32),
        compiler_params=params(0),
        cost_estimate=cost(1e6, 1.2e6),
        name="relation_out",
    )(rel_all)
    return entity_grad, relation_grad


def solution(mesh):
    in_specs = (
        P("ent", None),
        P("ent", None, None),
        P(("ent", "rel")),
        P(("ent", "rel")),
        P(("ent", "rel")),
        P(("ent", "rel")),
        P(("ent", "rel")),
        P("rel", None, None, None),
    )
    out_specs = (P("ent", None), P("rel", None, None, None))
    return jax.shard_map(local, mesh=mesh, in_specs=in_specs, out_specs=out_specs, check_vma=False)
```

```python
import functools

import jax
import jax.numpy as jnp
from jax import lax
from jax.experimental import pallas as pl
from jax.experimental.pallas import tpu as pltpu
from jax.sharding import PartitionSpec as P

F32 = jnp.float32
BF16 = jnp.bfloat16
TILE = 256
SMEM = pl.BlockSpec(memory_space=pltpu.SMEM)
ANY = pl.BlockSpec(memory_space=pl.ANY)
CONTRACT_LAST = (((1,), (1,)), ((), ()))


def iota(shape, axis):
    return lax.broadcasted_iota(jnp.int32, shape, axis)


def dot(a, b):
    return jnp.dot(a, b, preferred_element_type=F32)


def column(row):
    eye = iota((128, 128), 0) == iota((128, 128), 1)
    parts = []
    for k in range(row.shape[1] // 128):
        wide = jnp.broadcast_to(row[:, k * 128 : (k + 1) * 128].astype(F32), (128, 128))
        parts.append(jnp.sum(jnp.where(eye, wide, 0.0), axis=1, keepdims=True))
    return jnp.concatenate(parts, axis=0).astype(jnp.int32)


def hot_rows(col, width):
    return jnp.where(col == iota((col.shape[0], width), 1), 1.0, 0.0).astype(BF16)


def hot_columns(row, height):
    return jnp.where(row == iota((height, row.shape[1]), 0), 1.0, 0.0).astype(BF16)


def whole(shape):
    return pl.BlockSpec(shape, lambda *_: (0,) * len(shape))


def params(steps=1):
    return pltpu.CompilerParams(
        dimension_semantics=("arbitrary",) * (1 if steps else 0),
        vmem_limit_bytes=48 * 1024 * 1024,
    )


def cost(flops, nbytes):
    return pl.CostEstimate(flops=int(flops), bytes_accessed=int(nbytes), transcendentals=0)


def pick_kernel(share, scal, lists, table, after, out):
    n = lists.shape[0]
    slots = lists.shape[1]
    wide = jnp.broadcast_to(lists[...].astype(F32)[:, None, :], (n, share, slots))
    wide = wide.reshape(n * share, slots)
    shape = (n * share, slots)
    wanted = iota(shape, 1) == scal[0] * share + iota(shape, 0) % share
    col = jnp.sum(jnp.where(wanted, wide, 0.0), axis=1, keepdims=True).astype(jnp.int32)
    out[...] = dot(hot_rows(col, table.shape[0]), table[...]).astype(BF16)


def rows_kernel(share, rels, lists, after, out):
    n, slots = lists.shape
    wide = n * share
    ids = jnp.concatenate([lists[...], jnp.zeros((n, 128 - slots), jnp.int32)], axis=1)
    ids = jnp.concatenate([ids, jnp.zeros((128 - n, 128), jnp.int32)], axis=0)
    turned = ids.astype(F32).T.astype(jnp.int32)
    spread = jnp.where(iota((128, wide), 1) // share == iota((128, wide), 0), 1.0, 0.0)
    spread = spread.astype(BF16)
    low = dot((turned & 31).astype(F32).astype(BF16), spread)
    high = dot((turned >> 5).astype(F32).astype(BF16), spread)
    value = high * 32.0 + low
    slot = iota((128, wide), 0)
    for q in range(rels):
        wanted = slot == q * share + iota((128, wide), 1) % share
        out[q : q + 1, :] = jnp.sum(jnp.where(wanted, value, 0.0), axis=0, keepdims=True).astype(
            jnp.int32
        )


def head_kernel(
    r_count, blocks, scal, heads, rels, negs, table, ops,
    proj_out, negpart_out, turned_out, nege_out, bd_out, neg_rows, neg_acc,
):
    step = pl.program_id(0)
    d = table.shape[1]
    width = d // blocks
    n_neg = neg_rows.shape[0]

    @pl.when(step == 0)
    def _():
        spread = jnp.where(iota((width, d), 1) % width == iota((width, d), 0), 1.0, 0.0)
        spread = spread.astype(BF16)
        inside = iota((d, d), 0) // width == iota((d, d), 1) // width
        for r in range(r_count):
            full = dot(ops[r * d : (r + 1) * d, :], spread)
            bd_out[r * d : (r + 1) * d, :] = jnp.where(inside, full, 0.0).astype(BF16)
        neg_hot = hot_rows(column(negs[...]), table.shape[0])
        neg_rows[...] = dot(neg_hot, table[...]).astype(BF16)
        neg_acc[...] = jnp.zeros_like(neg_acc)

    head_wide = dot(hot_rows(column(heads[0]), table.shape[0]), table[...])
    head = head_wide.astype(BF16)
    turned_out[...] = head_wide.T.astype(BF16)
    rel_col = column(rels[0])
    proj = jnp.zeros((TILE, d), F32)
    for r in range(r_count):
        masked = jnp.where(rel_col == r, head_wide, 0.0).astype(BF16)
        proj = proj + dot(masked, bd_out[r * d : (r + 1) * d, :])
    proj = proj.astype(BF16)
    proj_out[...] = proj
    negative = lax.dot_general(proj, neg_rows[...], CONTRACT_LAST, preferred_element_type=F32)
    live = step * TILE + iota((TILE, n_neg), 0) < scal[1]
    weight = jnp.where(live, jax.nn.sigmoid(negative) / n_neg, 0.0)
    negpart_out[...] = dot(weight.astype(BF16), neg_rows[...])
    neg_acc[...] += dot(weight.T.astype(BF16), proj)

    @pl.when(step == pl.num_programs(0) - 1)
    def _():
        grads = neg_acc[...].astype(BF16)
        for k in range(table.shape[0] // TILE):
            hot = hot_columns(negs[...] - k * TILE, TILE)
            nege_out[k * TILE : (k + 1) * TILE, :] = dot(hot, grads)


def tail_kernel(n_rel, share, scal, tails, proj, negpart, *refs):
    chunks, (gp_out, *outs), (weighted, places) = (
        refs[:n_rel], refs[n_rel : 2 * n_rel + 1], refs[2 * n_rel + 1 :],
    )
    step = pl.program_id(0)
    rows = chunks[0].shape[0]
    slots = share * n_rel
    t = tails[0]
    slot = t % slots
    place = (slot // share - scal[0] + n_rel) % n_rel * rows
    place = place + t // slots * share + slot % share
    places[:, pl.ds(pl.multiple_of(step * TILE, TILE), TILE)] = place
    col = column(place)
    tail = jnp.zeros((TILE, proj.shape[1]), F32)
    for c in range(n_rel):
        tail = tail + dot(hot_rows(col - c * rows, rows), chunks[c][...])
    wide = proj[...].astype(F32)
    positive = jnp.sum(wide * tail, axis=1, keepdims=True)
    live = step * TILE + iota((TILE, 1), 0) < scal[1]
    pos_weight = jnp.where(live, -jax.nn.sigmoid(-positive), 0.0)
    gp_out[...] = (pos_weight * tail + negpart[...]).astype(BF16)
    weighted[pl.ds(pl.multiple_of(step * TILE, TILE), TILE), :] = (pos_weight * wide).astype(BF16)

    @pl.when(step == pl.num_programs(0) - 1)
    def _():
        for c in range(n_rel):
            for k in range(rows // TILE):
                hot = hot_columns(places[...] - (c * rows + k * TILE), TILE)
                outs[c][k * TILE : (k + 1) * TILE, :] = dot(hot, weighted[...]).astype(BF16)


def grad_kernel(
    blocks, n_rel, scal, heads, rels, gp, turned, nege, bd,
    rel_out, *refs,
):
    outs, (head_acc, rows_acc) = refs[:n_rel], refs[n_rel:]
    step = pl.program_id(0)
    edges, d = gp.shape
    width = d // blocks
    rel_row = rels[...]
    grads = gp[...]

    @pl.when(step == 0)
    def _():
        head_acc[...] = jnp.zeros_like(head_acc)

    masked = jnp.where(rel_row == step, turned[...].astype(F32), 0.0).astype(BF16)
    outer = dot(masked, grads)
    inside = iota((d, d), 0) // width == iota((d, d), 1) // width
    outer = jnp.where(inside, outer, 0.0)
    packed = outer[:width]
    for n in range(1, blocks):
        packed = packed + outer[n * width : (n + 1) * width]
    for half in range(d // 128):
        start = pl.multiple_of((half * pl.num_programs(0) + step) * width, width)
        rel_out[pl.ds(start, width), :] = packed[:, half * 128 : (half + 1) * 128].astype(BF16)
    for k in range(edges // TILE):
        part = pl.ds(k * TILE, TILE)
        rel_col = column(rel_row[:, k * TILE : (k + 1) * TILE])
        mine = jnp.where(rel_col == step, gp[part, :].astype(F32), 0.0).astype(BF16)
        head_acc[part, :] += lax.dot_general(mine, bd[...], CONTRACT_LAST, preferred_element_type=F32)

    @pl.when(step == pl.num_programs(0) - 1)
    def _():
        rows = nege.shape[0] // n_rel
        head_grad = head_acc[...].astype(BF16)
        for k in range(nege.shape[0] // TILE):
            part = slice(k * TILE, (k + 1) * TILE)
            rows_acc[part, :] = nege[part, :] + dot(hot_columns(heads[...] - k * TILE, TILE), head_grad)
        for c in range(n_rel):
            start = pl.multiple_of((scal[0] + c) % n_rel * rows, rows)
            outs[c][...] = rows_acc[pl.ds(start, rows), :].astype(BF16)


def owner_kernel(n_rel, scal, ids, *refs):
    shares, out = refs[:n_rel], refs[n_rel]
    step = pl.program_id(0)
    rows = out.shape[0]
    held = ids.shape[1]
    total = jnp.zeros(out.shape, F32)
    for c in range(n_rel):
        row = ids[pl.ds((scal[0] + c) % n_rel, 1), :]
        total = total + dot(hot_columns(row - step * rows, rows), shares[c][:held, :])
    for c in range(n_rel):
        @pl.when((scal[0] + c) % n_rel == step)
        def _(c=c):
            out[...] = total + shares[c][held:, :].astype(F32)


def relation_kernel(r_count, blocks, width, x, out):
    per = 128 // width
    for r in range(r_count):
        for n in range(blocks):
            start = (n // per * r_count + r) * width
            block = x[start : start + width, n % per * width : (n % per + 1) * width]
            out[r, n] = block.astype(F32)


def ring(x, n_rel, shift):
    return lax.ppermute(x, "rel", [((k + shift) % n_rel, k) for k in range(n_rel)])


def local(
    entity_rows, request_rows, edge_heads, edge_rels, edge_tails, edge_counts, negative_rows,
    relation_blocks,
):
    rows, d = entity_rows.shape
    parts, slots = request_rows.shape[1:]
    r_count, blocks, width = relation_blocks.shape[:3]
    edges, n_neg = edge_heads.shape[0], negative_rows.shape[0]
    n_rel = lax.axis_size("rel")
    share = slots // n_rel
    held = parts * share
    steps = edges // TILE
    me = lax.axis_index("rel").astype(jnp.int32)
    scal = jnp.concatenate([me.reshape(1), edge_counts])
    shaped = jax.ShapeDtypeStruct

    lists = lax.all_to_all(request_rows.reshape(parts, 1, slots), "ent", 0, 0, tiled=True)
    lists = lists.reshape(parts, slots)

    heads = edge_heads.reshape(steps, 1, TILE)
    rels = edge_rels.reshape(steps, 1, TILE)
    tails = edge_tails.reshape(steps, 1, TILE)
    negs = negative_rows.reshape(1, n_neg)
    id_block = pl.BlockSpec((1, 1, TILE), lambda i: (i, 0, 0))
    edge_block = pl.BlockSpec((TILE, d), lambda i: (i, 0))

    proj, negpart, turned, nege, bd = pl.pallas_call(
        functools.partial(head_kernel, r_count, blocks),
        grid=(steps,),
        in_specs=[
            SMEM, id_block, id_block, whole((1, n_neg)), whole((rows, d)),
            whole((r_count * d, width)),
        ],
        out_specs=[
            edge_block, edge_block, pl.BlockSpec((d, TILE), lambda i: (0, i)), whole((rows, d)),
            whole((r_count * d, d)),
        ],
        out_shape=[
            shaped((edges, d), BF16), shaped((edges, d), F32), shaped((d, edges), BF16),
            shaped((rows, d), F32), shaped((r_count * d, d), BF16),
        ],
        scratch_shapes=[pltpu.VMEM((n_neg, d), BF16), pltpu.VMEM((n_neg, d), F32)],
        compiler_params=params(),
        cost_estimate=cost(3e9, 6e6),
        name="head_step",
    )(scal, heads, rels, negs, entity_rows, relation_blocks.reshape(r_count * d, width))

    picked = pl.pallas_call(
        functools.partial(pick_kernel, share),
        in_specs=[SMEM, whole((parts, slots)), whole((rows, d)), ANY],
        out_specs=whole((held, d)),
        out_shape=shaped((held, d), BF16),
        compiler_params=params(0),
        cost_estimate=cost(2 * held * rows * d, 1e6),
        name="pick",
    )(scal, lists, entity_rows, nege)
    fetched = lax.all_to_all(picked, "ent", 0, 0, tiled=True)
    fetched = [fetched] + [ring(fetched, n_rel, c) for c in range(1, n_rel)]

    grad_proj, *slot_parts = pl.pallas_call(
        functools.partial(tail_kernel, n_rel, share),
        grid=(steps,),
        in_specs=[SMEM, id_block, edge_block, edge_block, ] + [whole((held, d))] * n_rel,
        out_specs=[edge_block] + [whole((held, d))] * n_rel,
        out_shape=[shaped((edges, d), BF16)] + [shaped((held, d), BF16)] * n_rel,
        scratch_shapes=[pltpu.VMEM((edges, d), BF16), pltpu.VMEM((1, edges), jnp.int32)],
        compiler_params=params(),
        cost_estimate=cost(3e9, 5e6),
        name="tail_step",
    )(scal, tails, proj, negpart, *fetched)
    list_rows = pl.pallas_call(
        functools.partial(rows_kernel, share, n_rel),
        in_specs=[whole((parts, slots)), ANY],
        out_specs=whole((n_rel, held)),
        out_shape=shaped((n_rel, held), jnp.int32),
        compiler_params=params(0),
        cost_estimate=cost(1e8, 1e5),
        name="list_rows",
    )(lists, grad_proj)
    slot_sum = slot_parts[0].astype(F32)
    for c in range(1, n_rel):
        slot_sum = slot_sum + ring(slot_parts[c], n_rel, n_rel - c).astype(F32)

    rel_part, *row_parts = pl.pallas_call(
        functools.partial(grad_kernel, blocks, n_rel),
        grid=(r_count,),
        in_specs=[
            SMEM, whole((1, edges)), whole((1, edges)), whole((edges, d)), whole((d, edges)),
            whole((rows, d)), pl.BlockSpec((d, d), lambda r: (r, 0)),
        ],
        out_specs=[whole((r_count * width * d // 128, 128))] + [whole((rows // n_rel, d))] * n_rel,
        out_shape=[shaped((r_count * width * d // 128, 128), BF16)]
        + [shaped((rows // n_rel, d), BF16)] * n_rel,
        scratch_shapes=[pltpu.VMEM((edges, d), F32), pltpu.VMEM((rows, d), F32)],
        compiler_params=params(),
        cost_estimate=cost(3e9, 6e6),
        name="grad_step",
    )(scal, edge_heads.reshape(1, edges), edge_rels.reshape(1, edges), grad_proj, turned, nege, bd)

    packed = jnp.concatenate([slot_sum.astype(BF16), rel_part], axis=1)
    returned = lax.all_to_all(packed, "ent", 0, 0, tiled=True)
    rel_sum = jnp.sum(returned[:, d:].reshape(parts, -1, 128).astype(F32), 0).astype(BF16)
    rel_all = jnp.broadcast_to(rel_sum[None], (parts,) + rel_sum.shape).reshape(-1, 128)
    rel_all = lax.all_to_all(rel_all, "ent", 0, 0, tiled=True)

    row_sum = row_parts[0].astype(F32)
    for c in range(1, n_rel):
        row_sum = row_sum + ring(row_parts[c], n_rel, n_rel - c).astype(F32)
    shares = jnp.concatenate([returned[:, :d], row_sum.astype(BF16)], axis=0)
    shares = [shares] + [ring(shares, n_rel, c) for c in range(1, n_rel)]

    entity_grad = pl.pallas_call(
        functools.partial(owner_kernel, n_rel),
        grid=(n_rel,),
        in_specs=[SMEM, whole((n_rel, held))] + [whole(shares[0].shape)] * n_rel,
        out_specs=pl.BlockSpec((rows // n_rel, d), lambda q: (q, 0)),
        out_shape=shaped((rows, d), F32),
        compiler_params=params(),
        cost_estimate=cost(1e9, 3e6),
        name="owner_add",
    )(scal, list_rows, *shares)
    relation_grad = pl.pallas_call(
        functools.partial(relation_kernel, r_count, blocks, width),
        in_specs=[whole(rel_all.shape)],
        out_specs=whole(relation_blocks.shape),
        out_shape=shaped(relation_blocks.shape, F32),
        compiler_params=params(0),
        cost_estimate=cost(1e6, 1.2e6),
        name="relation_out",
    )(rel_all)
    return entity_grad, relation_grad


def solution(mesh):
    in_specs = (
        P("ent", None),
        P("ent", None, None),
        P(("ent", "rel")),
        P(("ent", "rel")),
        P(("ent", "rel")),
        P(("ent", "rel")),
        P(("ent", "rel")),
        P("rel", None, None, None),
    )
    out_specs = (P("ent", None), P("rel", None, None, None))
    return jax.shard_map(local, mesh=mesh, in_specs=in_specs, out_specs=out_specs, check_vma=False)
```

```python
import functools

import jax
import jax.numpy as jnp
from jax import lax
from jax.experimental import pallas as pl
from jax.experimental.pallas import tpu as pltpu
from jax.sharding import PartitionSpec as P

F32 = jnp.float32
BF16 = jnp.bfloat16
TILE = 256
SMEM = pl.BlockSpec(memory_space=pltpu.SMEM)
ANY = pl.BlockSpec(memory_space=pl.ANY)
CONTRACT_LAST = (((1,), (1,)), ((), ()))


def iota(shape, axis):
    return lax.broadcasted_iota(jnp.int32, shape, axis)


def dot(a, b):
    return jnp.dot(a, b, preferred_element_type=F32)


def column(row):
    eye = iota((128, 128), 0) == iota((128, 128), 1)
    parts = []
    for k in range(row.shape[1] // 128):
        wide = jnp.broadcast_to(row[:, k * 128 : (k + 1) * 128].astype(F32), (128, 128))
        parts.append(jnp.sum(jnp.where(eye, wide, 0.0), axis=1, keepdims=True))
    return jnp.concatenate(parts, axis=0).astype(jnp.int32)


def hot_rows(col, width):
    return jnp.where(col == iota((col.shape[0], width), 1), 1.0, 0.0).astype(BF16)


def hot_columns(row, height):
    return jnp.where(row == iota((height, row.shape[1]), 0), 1.0, 0.0).astype(BF16)


def whole(shape):
    return pl.BlockSpec(shape, lambda *_: (0,) * len(shape))


def params(steps=1):
    return pltpu.CompilerParams(
        dimension_semantics=("arbitrary",) * (1 if steps else 0),
        vmem_limit_bytes=(24 if steps else 12) * 1024 * 1024,
    )


def cost(flops, nbytes):
    return pl.CostEstimate(flops=int(flops), bytes_accessed=int(nbytes), transcendentals=0)


def stage_kernel(table, out):
    out[...] = table[...]


def pick_kernel(share, scal, lists, table, out):
    n = lists.shape[0]
    slots = lists.shape[1]
    wide = jnp.broadcast_to(lists[...].astype(F32)[:, None, :], (n, share, slots))
    wide = wide.reshape(n * share, slots)
    shape = (n * share, slots)
    wanted = iota(shape, 1) == scal[0] * share + iota(shape, 0) % share
    col = jnp.sum(jnp.where(wanted, wide, 0.0), axis=1, keepdims=True).astype(jnp.int32)
    out[...] = dot(hot_rows(col, table.shape[0]), table[...]).astype(BF16)


def rows_kernel(share, scal, lists, after, out):
    n, slots = lists.shape
    wide = n * share
    ids = jnp.concatenate([lists[...], jnp.zeros((n, 128 - slots), jnp.int32)], axis=1)
    ids = jnp.concatenate([ids, jnp.zeros((128 - n, 128), jnp.int32)], axis=0)
    turned = ids.astype(F32).T.astype(jnp.int32)
    spread = jnp.where(iota((128, wide), 1) // share == iota((128, wide), 0), 1.0, 0.0)
    spread = spread.astype(BF16)
    low = dot((turned & 31).astype(F32).astype(BF16), spread)
    high = dot((turned >> 5).astype(F32).astype(BF16), spread)
    wanted = iota((128, wide), 0) == scal[0] * share + iota((128, wide), 1) % share
    value = jnp.where(wanted, high * 32.0 + low, 0.0)
    out[...] = jnp.sum(value, axis=0, keepdims=True).astype(jnp.int32)


def head_kernel(
    r_count, blocks, scal, heads, rels, negs, table, ops,
    proj_out, negpart_out, turned_out, nege_out, bd_out, neg_rows, neg_acc,
):
    step = pl.program_id(0)
    d = table.shape[1]
    width = d // blocks
    n_neg = neg_rows.shape[0]

    @pl.when(step == 0)
    def _():
        spread = jnp.where(iota((width, d), 1) % width == iota((width, d), 0), 1.0, 0.0)
        spread = spread.astype(BF16)
        inside = iota((d, d), 0) // width == iota((d, d), 1) // width
        for r in range(r_count):
            full = dot(ops[r * d : (r + 1) * d, :], spread)
            bd_out[r * d : (r + 1) * d, :] = jnp.where(inside, full, 0.0).astype(BF16)
        neg_hot = hot_rows(column(negs[...]), table.shape[0])
        neg_rows[...] = dot(neg_hot, table[...]).astype(BF16)
        neg_acc[...] = jnp.zeros_like(neg_acc)

    head_wide = dot(hot_rows(column(heads[0]), table.shape[0]), table[...])
    head = head_wide.astype(BF16)
    turned_out[...] = head_wide.T.astype(BF16)
    rel_col = column(rels[0])
    proj = jnp.zeros((TILE, d), F32)
    for r in range(r_count):
        masked = jnp.where(rel_col == r, head_wide, 0.0).astype(BF16)
        proj = proj + dot(masked, bd_out[r * d : (r + 1) * d, :])
    proj = proj.astype(BF16)
    proj_out[...] = proj
    negative = lax.dot_general(proj, neg_rows[...], CONTRACT_LAST, preferred_element_type=F32)
    live = step * TILE + iota((TILE, n_neg), 0) < scal[1]
    weight = jnp.where(live, jax.nn.sigmoid(negative) / n_neg, 0.0)
    negpart_out[...] = dot(weight.astype(BF16), neg_rows[...])
    neg_acc[...] += dot(weight.T.astype(BF16), proj)

    @pl.when(step == pl.num_programs(0) - 1)
    def _():
        grads = neg_acc[...].astype(BF16)
        for k in range(table.shape[0] // TILE):
            hot = hot_columns(negs[...] - k * TILE, TILE)
            nege_out[k * TILE : (k + 1) * TILE, :] = dot(hot, grads)


def tail_kernel(n_rel, share, scal, tails, proj, negpart, *refs):
    chunks, (gp_out, *outs), (weighted, places) = (
        refs[:n_rel], refs[n_rel : 2 * n_rel + 1], refs[2 * n_rel + 1 :],
    )
    step = pl.program_id(0)
    rows = chunks[0].shape[0]
    slots = share * n_rel
    t = tails[0]
    slot = t % slots
    place = (slot // share - scal[0] + n_rel) % n_rel * rows
    place = place + t // slots * share + slot % share
    places[:, pl.ds(pl.multiple_of(step * TILE, TILE), TILE)] = place
    col = column(place)
    tail = jnp.zeros((TILE, proj.shape[1]), F32)
    for c in range(n_rel):
        tail = tail + dot(hot_rows(col - c * rows, rows), chunks[c][...])
    wide = proj[...].astype(F32)
    positive = jnp.sum(wide * tail, axis=1, keepdims=True)
    live = step * TILE + iota((TILE, 1), 0) < scal[1]
    pos_weight = jnp.where(live, -jax.nn.sigmoid(-positive), 0.0)
    gp_out[...] = (pos_weight * tail + negpart[...]).astype(BF16)
    weighted[pl.ds(pl.multiple_of(step * TILE, TILE), TILE), :] = (pos_weight * wide).astype(BF16)

    @pl.when(step == pl.num_programs(0) - 1)
    def _():
        for c in range(n_rel):
            for k in range(rows // TILE):
                hot = hot_columns(places[...] - (c * rows + k * TILE), TILE)
                outs[c][k * TILE : (k + 1) * TILE, :] = dot(hot, weighted[...]).astype(BF16)


def grad_kernel(
    blocks, heads, rels, gp, turned, nege, bd,
    rel_out, rows_out, head_acc,
):
    step = pl.program_id(0)
    edges, d = gp.shape
    width = d // blocks
    rel_row = rels[...]
    grads = gp[...]

    @pl.when(step == 0)
    def _():
        head_acc[...] = jnp.zeros_like(head_acc)

    masked = jnp.where(rel_row == step, turned[...].astype(F32), 0.0).astype(BF16)
    outer = dot(masked, grads)
    inside = iota((d, d), 0) // width == iota((d, d), 1) // width
    outer = jnp.where(inside, outer, 0.0)
    packed = outer[:width]
    for n in range(1, blocks):
        packed = packed + outer[n * width : (n + 1) * width]
    for half in range(d // 128):
        start = pl.multiple_of((half * pl.num_programs(0) + step) * width, width)
        rel_out[pl.ds(start, width), :] = packed[:, half * 128 : (half + 1) * 128].astype(BF16)
    for k in range(edges // TILE):
        part = pl.ds(k * TILE, TILE)
        rel_col = column(rel_row[:, k * TILE : (k + 1) * TILE])
        mine = jnp.where(rel_col == step, gp[part, :].astype(F32), 0.0).astype(BF16)
        head_acc[part, :] += lax.dot_general(mine, bd[...], CONTRACT_LAST, preferred_element_type=F32)

    @pl.when(step == pl.num_programs(0) - 1)
    def _():
        head_grad = head_acc[...].astype(BF16)
        for k in range(nege.shape[0] // TILE):
            part = slice(k * TILE, (k + 1) * TILE)
            rows_out[part, :] = nege[part, :] + dot(hot_columns(heads[...] - k * TILE, TILE), head_grad)


def owner_kernel(n_rel, scal, ids, returned, terms, *outs):
    d = terms.shape[1]
    rows = terms.shape[0] // n_rel
    for c in range(n_rel):
        start = pl.multiple_of((scal[0] + c) % n_rel * rows, rows)
        total = terms[pl.ds(start, rows), :]
        total = total + dot(hot_columns(ids[...] - start, rows), returned[:, :d])
        outs[c][...] = total.astype(BF16)


def place_kernel(n_rel, scal, *refs):
    out = refs[n_rel]
    rows = out.shape[0] // n_rel
    for c in range(n_rel):
        start = pl.multiple_of((scal[0] + c) % n_rel * rows, rows)
        out[pl.ds(start, rows), :] = refs[c][...].astype(F32)


def relation_kernel(r_count, blocks, width, x, out):
    per = 128 // width
    for r in range(r_count):
        for n in range(blocks):
            start = (n // per * r_count + r) * width
            block = x[start : start + width, n % per * width : (n % per + 1) * width]
            out[r, n] = block.astype(F32)


def ring(x, n_rel, shift):
    return lax.ppermute(x, "rel", [((k + shift) % n_rel, k) for k in range(n_rel)])


def local(
    entity_rows, request_rows, edge_heads, edge_rels, edge_tails, edge_counts, negative_rows,
    relation_blocks,
):
    rows, d = entity_rows.shape
    parts, slots = request_rows.shape[1:]
    r_count, blocks, width = relation_blocks.shape[:3]
    edges, n_neg = edge_heads.shape[0], negative_rows.shape[0]
    n_rel = lax.axis_size("rel")
    share = slots // n_rel
    held = parts * share
    steps = edges // TILE
    me = lax.axis_index("rel").astype(jnp.int32)
    scal = jnp.concatenate([me.reshape(1), edge_counts])
    shaped = jax.ShapeDtypeStruct

    lists = lax.all_to_all(request_rows.reshape(parts, 1, slots), "ent", 0, 0, tiled=True)
    lists = lists.reshape(parts, slots)

    heads = edge_heads.reshape(steps, 1, TILE)
    rels = edge_rels.reshape(steps, 1, TILE)
    tails = edge_tails.reshape(steps, 1, TILE)
    negs = negative_rows.reshape(1, n_neg)
    id_block = pl.BlockSpec((1, 1, TILE), lambda i: (i, 0, 0))
    edge_block = pl.BlockSpec((TILE, d), lambda i: (i, 0))

    table = pl.pallas_call(
        stage_kernel,
        in_specs=[whole((rows, d))],
        out_specs=whole((rows, d)),
        out_shape=shaped((rows, d), BF16),
        compiler_params=params(0),
        cost_estimate=cost(1e6, 1e6),
        name="stage",
    )(entity_rows)
    picked = pl.pallas_call(
        functools.partial(pick_kernel, share),
        in_specs=[SMEM, whole((parts, slots)), whole((rows, d))],
        out_specs=whole((held, d)),
        out_shape=shaped((held, d), BF16),
        compiler_params=params(0),
        cost_estimate=cost(2 * held * rows * d, 1e6),
        name="pick",
    )(scal, lists, table)
    proj, negpart, turned, nege, bd = pl.pallas_call(
        functools.partial(head_kernel, r_count, blocks),
        grid=(steps,),
        in_specs=[
            SMEM, id_block, id_block, whole((1, n_neg)), whole((rows, d)),
            whole((r_count * d, width)),
        ],
        out_specs=[
            edge_block, edge_block, pl.BlockSpec((d, TILE), lambda i: (0, i)), whole((rows, d)),
            whole((r_count * d, d)),
        ],
        out_shape=[
            shaped((edges, d), BF16), shaped((edges, d), F32), shaped((d, edges), BF16),
            shaped((rows, d), F32), shaped((r_count * d, d), BF16),
        ],
        scratch_shapes=[pltpu.VMEM((n_neg, d), BF16), pltpu.VMEM((n_neg, d), F32)],
        compiler_params=params(),
        cost_estimate=cost(3e9, 6e6),
        name="head_step",
    )(scal, heads, rels, negs, entity_rows, relation_blocks.reshape(r_count * d, width))

    fetched = lax.all_to_all(picked, "ent", 0, 0, tiled=True)
    fetched = [fetched] + [ring(fetched, n_rel, c) for c in range(1, n_rel)]

    grad_proj, *slot_parts = pl.pallas_call(
        functools.partial(tail_kernel, n_rel, share),
        grid=(steps,),
        in_specs=[SMEM, id_block, edge_block, edge_block, ] + [whole((held, d))] * n_rel,
        out_specs=[edge_block] + [whole((held, d))] * n_rel,
        out_shape=[shaped((edges, d), BF16)] + [shaped((held, d), BF16)] * n_rel,
        scratch_shapes=[pltpu.VMEM((edges, d), BF16), pltpu.VMEM((1, edges), jnp.int32)],
        compiler_params=params(),
        cost_estimate=cost(3e9, 5e6),
        name="tail_step",
    )(scal, tails, proj, negpart, *fetched)
    list_rows = pl.pallas_call(
        functools.partial(rows_kernel, share),
        in_specs=[SMEM, whole((parts, slots)), ANY],
        out_specs=whole((1, held)),
        out_shape=shaped((1, held), jnp.int32),
        compiler_params=params(0),
        cost_estimate=cost(1e8, 1e5),
        name="list_rows",
    )(scal, lists, grad_proj)
    slot_sum = slot_parts[0].astype(F32)
    for c in range(1, n_rel):
        slot_sum = slot_sum + ring(slot_parts[c], n_rel, n_rel - c).astype(F32)

    rel_part, row_terms = pl.pallas_call(
        functools.partial(grad_kernel, blocks),
        grid=(r_count,),
        in_specs=[
            whole((1, edges)), whole((1, edges)), whole((edges, d)), whole((d, edges)),
            whole((rows, d)), pl.BlockSpec((d, d), lambda r: (r, 0)),
        ],
        out_specs=[whole((r_count * width * d // 128, 128)), whole((rows, d))],
        out_shape=[shaped((r_count * width * d // 128, 128), BF16), shaped((rows, d), F32)],
        scratch_shapes=[pltpu.VMEM((edges, d), F32)],
        compiler_params=params(),
        cost_estimate=cost(3e9, 6e6),
        name="grad_step",
    )(edge_heads.reshape(1, edges), edge_rels.reshape(1, edges), grad_proj, turned, nege, bd)

    packed = jnp.concatenate([slot_sum.astype(BF16), rel_part], axis=1)
    returned = lax.all_to_all(packed, "ent", 0, 0, tiled=True)
    rel_sum = jnp.sum(returned[:, d:].reshape(parts, -1, 128).astype(F32), 0).astype(BF16)
    rel_all = jnp.broadcast_to(rel_sum[None], (parts,) + rel_sum.shape).reshape(-1, 128)
    rel_all = lax.all_to_all(rel_all, "ent", 0, 0, tiled=True)

    row_parts = pl.pallas_call(
        functools.partial(owner_kernel, n_rel),
        in_specs=[SMEM, whole((1, held)), whole(returned.shape), whole((rows, d))],
        out_specs=[whole((rows // n_rel, d))] * n_rel,
        out_shape=[shaped((rows // n_rel, d), BF16)] * n_rel,
        compiler_params=params(0),
        cost_estimate=cost(3e8, 2e6),
        name="owner_add",
    )(scal, list_rows, returned, row_terms)
    row_sum = row_parts[0].astype(F32)
    for c in range(1, n_rel):
        row_sum = row_sum + ring(row_parts[c], n_rel, n_rel - c).astype(F32)
    row_sum = row_sum.astype(BF16)
    row_sums = [row_sum] + [ring(row_sum, n_rel, c) for c in range(1, n_rel)]
    entity_grad = pl.pallas_call(
        functools.partial(place_kernel, n_rel),
        in_specs=[SMEM] + [whole((rows // n_rel, d))] * n_rel,
        out_specs=whole((rows, d)),
        out_shape=shaped((rows, d), F32),
        compiler_params=params(0),
        cost_estimate=cost(1e6, 1.5e6),
        name="place_rows",
    )(scal, *row_sums)
    rel_all, entity_grad = lax.optimization_barrier((rel_all, entity_grad))
    relation_grad = pl.pallas_call(
        functools.partial(relation_kernel, r_count, blocks, width),
        in_specs=[whole(rel_all.shape)],
        out_specs=whole(relation_blocks.shape),
        out_shape=shaped(relation_blocks.shape, F32),
        compiler_params=params(0),
        cost_estimate=cost(1e6, 1.2e6),
        name="relation_out",
    )(rel_all)
    return entity_grad, relation_grad


def solution(mesh):
    in_specs = (
        P("ent", None),
        P("ent", None, None),
        P(("ent", "rel")),
        P(("ent", "rel")),
        P(("ent", "rel")),
        P(("ent", "rel")),
        P(("ent", "rel")),
        P("rel", None, None, None),
    )
    out_specs = (P("ent", None), P("rel", None, None, None))
    return jax.shard_map(local, mesh=mesh, in_specs=in_specs, out_specs=out_specs, check_vma=False)
```

```python
import functools

import jax
import jax.numpy as jnp
from jax import lax
from jax.experimental import pallas as pl
from jax.experimental.pallas import tpu as pltpu
from jax.sharding import PartitionSpec as P

F32 = jnp.float32
BF16 = jnp.bfloat16
TILE = 512
SMEM = pl.BlockSpec(memory_space=pltpu.SMEM)
ANY = pl.BlockSpec(memory_space=pl.ANY)
CONTRACT_LAST = (((1,), (1,)), ((), ()))


def iota(shape, axis):
    return lax.broadcasted_iota(jnp.int32, shape, axis)


def dot(a, b):
    return jnp.dot(a, b, preferred_element_type=F32)


def column(row):
    eye = iota((128, 128), 0) == iota((128, 128), 1)
    parts = []
    for k in range(row.shape[1] // 128):
        wide = jnp.broadcast_to(row[:, k * 128 : (k + 1) * 128].astype(F32), (128, 128))
        parts.append(jnp.sum(jnp.where(eye, wide, 0.0), axis=1, keepdims=True))
    return jnp.concatenate(parts, axis=0).astype(jnp.int32)


def hot_rows(col, width):
    return jnp.where(col == iota((col.shape[0], width), 1), 1.0, 0.0).astype(BF16)


def hot_columns(row, height):
    return jnp.where(row == iota((height, row.shape[1]), 0), 1.0, 0.0).astype(BF16)


def whole(shape):
    return pl.BlockSpec(shape, lambda *_: (0,) * len(shape))


def params(steps=1):
    return pltpu.CompilerParams(
        dimension_semantics=("arbitrary",) * (1 if steps else 0),
        vmem_limit_bytes=(24 if steps else 12) * 1024 * 1024,
    )


def cost(flops, nbytes):
    return pl.CostEstimate(flops=int(flops), bytes_accessed=int(nbytes), transcendentals=0)


def stage_kernel(table, out):
    out[...] = table[...]


def pick_kernel(share, scal, lists, table, out):
    n = lists.shape[0]
    slots = lists.shape[1]
    wide = jnp.broadcast_to(lists[...].astype(F32)[:, None, :], (n, share, slots))
    wide = wide.reshape(n * share, slots)
    shape = (n * share, slots)
    wanted = iota(shape, 1) == scal[0] * share + iota(shape, 0) % share
    col = jnp.sum(jnp.where(wanted, wide, 0.0), axis=1, keepdims=True).astype(jnp.int32)
    out[...] = dot(hot_rows(col, table.shape[0]), table[...]).astype(BF16)


def rows_kernel(share, scal, lists, after, out):
    n, slots = lists.shape
    wide = n * share
    ids = jnp.concatenate([lists[...], jnp.zeros((n, 128 - slots), jnp.int32)], axis=1)
    ids = jnp.concatenate([ids, jnp.zeros((128 - n, 128), jnp.int32)], axis=0)
    turned = ids.astype(F32).T.astype(jnp.int32)
    spread = jnp.where(iota((128, wide), 1) // share == iota((128, wide), 0), 1.0, 0.0)
    spread = spread.astype(BF16)
    low = dot((turned & 31).astype(F32).astype(BF16), spread)
    high = dot((turned >> 5).astype(F32).astype(BF16), spread)
    wanted = iota((128, wide), 0) == scal[0] * share + iota((128, wide), 1) % share
    value = jnp.where(wanted, high * 32.0 + low, 0.0)
    out[...] = jnp.sum(value, axis=0, keepdims=True).astype(jnp.int32)


def head_kernel(
    r_count, blocks, scal, heads, rels, negs, table, ops,
    proj_out, negpart_out, turned_out, nege_out, bd_out, neg_rows, neg_acc,
):
    step = pl.program_id(0)
    d = table.shape[1]
    width = d // blocks
    n_neg = neg_rows.shape[0]

    @pl.when(step == 0)
    def _():
        spread = jnp.where(iota((width, d), 1) % width == iota((width, d), 0), 1.0, 0.0)
        spread = spread.astype(BF16)
        inside = iota((d, d), 0) // width == iota((d, d), 1) // width
        for r in range(r_count):
            full = dot(ops[r * d : (r + 1) * d, :], spread)
            bd_out[r * d : (r + 1) * d, :] = jnp.where(inside, full, 0.0).astype(BF16)
        neg_hot = hot_rows(column(negs[...]), table.shape[0])
        neg_rows[...] = dot(neg_hot, table[...]).astype(BF16)
        neg_acc[...] = jnp.zeros_like(neg_acc)

    head_wide = dot(hot_rows(column(heads[0]), table.shape[0]), table[...])
    head = head_wide.astype(BF16)
    turned_out[...] = head_wide.T.astype(BF16)
    rel_col = column(rels[0])
    proj = jnp.zeros((TILE, d), F32)
    for r in range(r_count):
        masked = jnp.where(rel_col == r, head_wide, 0.0).astype(BF16)
        proj = proj + dot(masked, bd_out[r * d : (r + 1) * d, :])
    proj = proj.astype(BF16)
    proj_out[...] = proj
    negative = lax.dot_general(proj, neg_rows[...], CONTRACT_LAST, preferred_element_type=F32)
    live = step * TILE + iota((TILE, n_neg), 0) < scal[1]
    weight = jnp.where(live, jax.nn.sigmoid(negative) / n_neg, 0.0)
    negpart_out[...] = dot(weight.astype(BF16), neg_rows[...])
    neg_acc[...] += dot(weight.T.astype(BF16), proj)

    @pl.when(step == pl.num_programs(0) - 1)
    def _():
        grads = neg_acc[...].astype(BF16)
        for k in range(table.shape[0] // TILE):
            hot = hot_columns(negs[...] - k * TILE, TILE)
            nege_out[k * TILE : (k + 1) * TILE, :] = dot(hot, grads)


def tail_kernel(n_rel, share, scal, tails, proj, negpart, *refs):
    chunks, (gp_out, *outs), (weighted, places) = (
        refs[:n_rel], refs[n_rel : 2 * n_rel + 1], refs[2 * n_rel + 1 :],
    )
    step = pl.program_id(0)
    rows = chunks[0].shape[0]
    slots = share * n_rel
    t = tails[0]
    slot = t % slots
    place = (slot // share - scal[0] + n_rel) % n_rel * rows
    place = place + t // slots * share + slot % share
    places[:, pl.ds(pl.multiple_of(step * TILE, TILE), TILE)] = place
    col = column(place)
    tail = jnp.zeros((TILE, proj.shape[1]), F32)
    for c in range(n_rel):
        tail = tail + dot(hot_rows(col - c * rows, rows), chunks[c][...])
    wide = proj[...].astype(F32)
    positive = jnp.sum(wide * tail, axis=1, keepdims=True)
    live = step * TILE + iota((TILE, 1), 0) < scal[1]
    pos_weight = jnp.where(live, -jax.nn.sigmoid(-positive), 0.0)
    gp_out[...] = (pos_weight * tail + negpart[...]).astype(BF16)
    weighted[pl.ds(pl.multiple_of(step * TILE, TILE), TILE), :] = (pos_weight * wide).astype(BF16)

    @pl.when(step == pl.num_programs(0) - 1)
    def _():
        for c in range(n_rel):
            for k in range(rows // TILE):
                hot = hot_columns(places[...] - (c * rows + k * TILE), TILE)
                outs[c][k * TILE : (k + 1) * TILE, :] = dot(hot, weighted[...]).astype(BF16)


def grad_kernel(
    blocks, heads, rels, gp, turned, nege, bd,
    rel_out, rows_out, head_acc,
):
    step = pl.program_id(0)
    edges, d = gp.shape
    width = d // blocks
    rel_row = rels[...]
    grads = gp[...]

    @pl.when(step == 0)
    def _():
        head_acc[...] = jnp.zeros_like(head_acc)

    masked = jnp.where(rel_row == step, turned[...].astype(F32), 0.0).astype(BF16)
    outer = dot(masked, grads)
    inside = iota((d, d), 0) // width == iota((d, d), 1) // width
    outer = jnp.where(inside, outer, 0.0)
    packed = outer[:width]
    for n in range(1, blocks):
        packed = packed + outer[n * width : (n + 1) * width]
    for half in range(d // 128):
        start = pl.multiple_of((half * pl.num_programs(0) + step) * width, width)
        rel_out[pl.ds(start, width), :] = packed[:, half * 128 : (half + 1) * 128].astype(BF16)
    for k in range(edges // TILE):
        part = pl.ds(k * TILE, TILE)
        rel_col = column(rel_row[:, k * TILE : (k + 1) * TILE])
        mine = jnp.where(rel_col == step, gp[part, :].astype(F32), 0.0).astype(BF16)
        head_acc[part, :] += lax.dot_general(mine, bd[...], CONTRACT_LAST, preferred_element_type=F32)

    @pl.when(step == pl.num_programs(0) - 1)
    def _():
        head_grad = head_acc[...].astype(BF16)
        for k in range(nege.shape[0] // TILE):
            part = slice(k * TILE, (k + 1) * TILE)
            rows_out[part, :] = nege[part, :] + dot(hot_columns(heads[...] - k * TILE, TILE), head_grad)


def owner_kernel(n_rel, scal, ids, returned, terms, *outs):
    d = terms.shape[1]
    rows = terms.shape[0] // n_rel
    for c in range(n_rel):
        start = pl.multiple_of((scal[0] + c) % n_rel * rows, rows)
        total = terms[pl.ds(start, rows), :]
        total = total + dot(hot_columns(ids[...] - start, rows), returned[:, :d])
        outs[c][...] = total.astype(BF16)


def place_kernel(n_rel, scal, *refs):
    out = refs[n_rel]
    rows = out.shape[0] // n_rel
    for c in range(n_rel):
        start = pl.multiple_of((scal[0] + c) % n_rel * rows, rows)
        out[pl.ds(start, rows), :] = refs[c][...].astype(F32)


def relation_kernel(r_count, blocks, width, x, out):
    per = 128 // width
    for r in range(r_count):
        for n in range(blocks):
            start = (n // per * r_count + r) * width
            block = x[start : start + width, n % per * width : (n % per + 1) * width]
            out[r, n] = block.astype(F32)


def ring(x, n_rel, shift):
    return lax.ppermute(x, "rel", [((k + shift) % n_rel, k) for k in range(n_rel)])


def local(
    entity_rows, request_rows, edge_heads, edge_rels, edge_tails, edge_counts, negative_rows,
    relation_blocks,
):
    rows, d = entity_rows.shape
    parts, slots = request_rows.shape[1:]
    r_count, blocks, width = relation_blocks.shape[:3]
    edges, n_neg = edge_heads.shape[0], negative_rows.shape[0]
    n_rel = lax.axis_size("rel")
    share = slots // n_rel
    held = parts * share
    steps = edges // TILE
    me = lax.axis_index("rel").astype(jnp.int32)
    scal = jnp.concatenate([me.reshape(1), edge_counts])
    shaped = jax.ShapeDtypeStruct

    lists = lax.all_to_all(request_rows.reshape(parts, 1, slots), "ent", 0, 0, tiled=True)
    lists = lists.reshape(parts, slots)

    heads = edge_heads.reshape(steps, 1, TILE)
    rels = edge_rels.reshape(steps, 1, TILE)
    tails = edge_tails.reshape(steps, 1, TILE)
    negs = negative_rows.reshape(1, n_neg)
    id_block = pl.BlockSpec((1, 1, TILE), lambda i: (i, 0, 0))
    edge_block = pl.BlockSpec((TILE, d), lambda i: (i, 0))

    table = pl.pallas_call(
        stage_kernel,
        in_specs=[whole((rows, d))],
        out_specs=whole((rows, d)),
        out_shape=shaped((rows, d), BF16),
        compiler_params=params(0),
        cost_estimate=cost(1e6, 1e6),
        name="stage",
    )(entity_rows)
    picked = pl.pallas_call(
        functools.partial(pick_kernel, share),
        in_specs=[SMEM, whole((parts, slots)), whole((rows, d))],
        out_specs=whole((held, d)),
        out_shape=shaped((held, d), BF16),
        compiler_params=params(0),
        cost_estimate=cost(2 * held * rows * d, 1e6),
        name="pick",
    )(scal, lists, table)
    proj, negpart, turned, nege, bd = pl.pallas_call(
        functools.partial(head_kernel, r_count, blocks),
        grid=(steps,),
        in_specs=[
            SMEM, id_block, id_block, whole((1, n_neg)), whole((rows, d)),
            whole((r_count * d, width)),
        ],
        out_specs=[
            edge_block, edge_block, pl.BlockSpec((d, TILE), lambda i: (0, i)), whole((rows, d)),
            whole((r_count * d, d)),
        ],
        out_shape=[
            shaped((edges, d), BF16), shaped((edges, d), F32), shaped((d, edges), BF16),
            shaped((rows, d), F32), shaped((r_count * d, d), BF16),
        ],
        scratch_shapes=[pltpu.VMEM((n_neg, d), BF16), pltpu.VMEM((n_neg, d), F32)],
        compiler_params=params(),
        cost_estimate=cost(3e9, 6e6),
        name="head_step",
    )(scal, heads, rels, negs, entity_rows, relation_blocks.reshape(r_count * d, width))

    fetched = lax.all_to_all(picked, "ent", 0, 0, tiled=True)
    fetched = [fetched] + [ring(fetched, n_rel, c) for c in range(1, n_rel)]

    grad_proj, *slot_parts = pl.pallas_call(
        functools.partial(tail_kernel, n_rel, share),
        grid=(steps,),
        in_specs=[SMEM, id_block, edge_block, edge_block, ] + [whole((held, d))] * n_rel,
        out_specs=[edge_block] + [whole((held, d))] * n_rel,
        out_shape=[shaped((edges, d), BF16)] + [shaped((held, d), BF16)] * n_rel,
        scratch_shapes=[pltpu.VMEM((edges, d), BF16), pltpu.VMEM((1, edges), jnp.int32)],
        compiler_params=params(),
        cost_estimate=cost(3e9, 5e6),
        name="tail_step",
    )(scal, tails, proj, negpart, *fetched)
    list_rows = pl.pallas_call(
        functools.partial(rows_kernel, share),
        in_specs=[SMEM, whole((parts, slots)), ANY],
        out_specs=whole((1, held)),
        out_shape=shaped((1, held), jnp.int32),
        compiler_params=params(0),
        cost_estimate=cost(1e8, 1e5),
        name="list_rows",
    )(scal, lists, grad_proj)
    slot_sum = slot_parts[0].astype(F32)
    for c in range(1, n_rel):
        slot_sum = slot_sum + ring(slot_parts[c], n_rel, n_rel - c).astype(F32)

    rel_part, row_terms = pl.pallas_call(
        functools.partial(grad_kernel, blocks),
        grid=(r_count,),
        in_specs=[
            whole((1, edges)), whole((1, edges)), whole((edges, d)), whole((d, edges)),
            whole((rows, d)), pl.BlockSpec((d, d), lambda r: (r, 0)),
        ],
        out_specs=[whole((r_count * width * d // 128, 128)), whole((rows, d))],
        out_shape=[shaped((r_count * width * d // 128, 128), BF16), shaped((rows, d), F32)],
        scratch_shapes=[pltpu.VMEM((edges, d), F32)],
        compiler_params=params(),
        cost_estimate=cost(3e9, 6e6),
        name="grad_step",
    )(edge_heads.reshape(1, edges), edge_rels.reshape(1, edges), grad_proj, turned, nege, bd)

    packed = jnp.concatenate([slot_sum.astype(BF16), rel_part], axis=1)
    returned = lax.all_to_all(packed, "ent", 0, 0, tiled=True)
    rel_sum = jnp.sum(returned[:, d:].reshape(parts, -1, 128).astype(F32), 0).astype(BF16)
    rel_all = jnp.broadcast_to(rel_sum[None], (parts,) + rel_sum.shape).reshape(-1, 128)
    rel_all = lax.all_to_all(rel_all, "ent", 0, 0, tiled=True)

    row_parts = pl.pallas_call(
        functools.partial(owner_kernel, n_rel),
        in_specs=[SMEM, whole((1, held)), whole(returned.shape), whole((rows, d))],
        out_specs=[whole((rows // n_rel, d))] * n_rel,
        out_shape=[shaped((rows // n_rel, d), BF16)] * n_rel,
        compiler_params=params(0),
        cost_estimate=cost(3e8, 2e6),
        name="owner_add",
    )(scal, list_rows, returned, row_terms)
    row_sum = row_parts[0].astype(F32)
    for c in range(1, n_rel):
        row_sum = row_sum + ring(row_parts[c], n_rel, n_rel - c).astype(F32)
    row_sum = row_sum.astype(BF16)
    row_sums = [row_sum] + [ring(row_sum, n_rel, c) for c in range(1, n_rel)]
    entity_grad = pl.pallas_call(
        functools.partial(place_kernel, n_rel),
        in_specs=[SMEM] + [whole((rows // n_rel, d))] * n_rel,
        out_specs=whole((rows, d)),
        out_shape=shaped((rows, d), F32),
        compiler_params=params(0),
        cost_estimate=cost(1e6, 1.5e6),
        name="place_rows",
    )(scal, *row_sums)
    rel_all, entity_grad = lax.optimization_barrier((rel_all, entity_grad))
    relation_grad = pl.pallas_call(
        functools.partial(relation_kernel, r_count, blocks, width),
        in_specs=[whole(rel_all.shape)],
        out_specs=whole(relation_blocks.shape),
        out_shape=shaped(relation_blocks.shape, F32),
        compiler_params=params(0),
        cost_estimate=cost(1e6, 1.2e6),
        name="relation_out",
    )(rel_all)
    return entity_grad, relation_grad


def solution(mesh):
    in_specs = (
        P("ent", None),
        P("ent", None, None),
        P(("ent", "rel")),
        P(("ent", "rel")),
        P(("ent", "rel")),
        P(("ent", "rel")),
        P(("ent", "rel")),
        P("rel", None, None, None),
    )
    out_specs = (P("ent", None), P("rel", None, None, None))
    return jax.shard_map(local, mesh=mesh, in_specs=in_specs, out_specs=out_specs, check_vma=False)
```

```python
import functools

import jax
import jax.numpy as jnp
from jax import lax
from jax.experimental import pallas as pl
from jax.experimental.pallas import tpu as pltpu
from jax.sharding import PartitionSpec as P

F32 = jnp.float32
BF16 = jnp.bfloat16
TILE = 1024
SMEM = pl.BlockSpec(memory_space=pltpu.SMEM)
ANY = pl.BlockSpec(memory_space=pl.ANY)
CONTRACT_LAST = (((1,), (1,)), ((), ()))


def iota(shape, axis):
    return lax.broadcasted_iota(jnp.int32, shape, axis)


def dot(a, b):
    return jnp.dot(a, b, preferred_element_type=F32)


def column(row):
    eye = iota((128, 128), 0) == iota((128, 128), 1)
    parts = []
    for k in range(row.shape[1] // 128):
        wide = jnp.broadcast_to(row[:, k * 128 : (k + 1) * 128].astype(F32), (128, 128))
        parts.append(jnp.sum(jnp.where(eye, wide, 0.0), axis=1, keepdims=True))
    return jnp.concatenate(parts, axis=0).astype(jnp.int32)


def hot_rows(col, width):
    return jnp.where(col == iota((col.shape[0], width), 1), 1.0, 0.0).astype(BF16)


def hot_columns(row, height):
    return jnp.where(row == iota((height, row.shape[1]), 0), 1.0, 0.0).astype(BF16)


def whole(shape):
    return pl.BlockSpec(shape, lambda *_: (0,) * len(shape))


def params(steps=1):
    return pltpu.CompilerParams(
        dimension_semantics=("arbitrary",) * (1 if steps else 0),
        vmem_limit_bytes=(24 if steps else 12) * 1024 * 1024,
    )


def cost(flops, nbytes):
    return pl.CostEstimate(flops=int(flops), bytes_accessed=int(nbytes), transcendentals=0)


def stage_kernel(table, out):
    out[...] = table[...]


def pick_kernel(share, scal, lists, table, out):
    n = lists.shape[0]
    slots = lists.shape[1]
    wide = jnp.broadcast_to(lists[...].astype(F32)[:, None, :], (n, share, slots))
    wide = wide.reshape(n * share, slots)
    shape = (n * share, slots)
    wanted = iota(shape, 1) == scal[0] * share + iota(shape, 0) % share
    col = jnp.sum(jnp.where(wanted, wide, 0.0), axis=1, keepdims=True).astype(jnp.int32)
    out[...] = dot(hot_rows(col, table.shape[0]), table[...]).astype(BF16)


def rows_kernel(share, scal, lists, after, out):
    n, slots = lists.shape
    wide = n * share
    ids = jnp.concatenate([lists[...], jnp.zeros((n, 128 - slots), jnp.int32)], axis=1)
    ids = jnp.concatenate([ids, jnp.zeros((128 - n, 128), jnp.int32)], axis=0)
    turned = ids.astype(F32).T.astype(jnp.int32)
    spread = jnp.where(iota((128, wide), 1) // share == iota((128, wide), 0), 1.0, 0.0)
    spread = spread.astype(BF16)
    low = dot((turned & 31).astype(F32).astype(BF16), spread)
    high = dot((turned >> 5).astype(F32).astype(BF16), spread)
    wanted = iota((128, wide), 0) == scal[0] * share + iota((128, wide), 1) % share
    value = jnp.where(wanted, high * 32.0 + low, 0.0)
    out[...] = jnp.sum(value, axis=0, keepdims=True).astype(jnp.int32)


def head_kernel(
    r_count, blocks, scal, heads, rels, negs, table, ops,
    proj_out, negpart_out, turned_out, nege_out, bd_out, neg_rows, neg_acc,
):
    step = pl.program_id(0)
    d = table.shape[1]
    width = d // blocks
    n_neg = neg_rows.shape[0]

    @pl.when(step == 0)
    def _():
        spread = jnp.where(iota((width, d), 1) % width == iota((width, d), 0), 1.0, 0.0)
        spread = spread.astype(BF16)
        inside = iota((d, d), 0) // width == iota((d, d), 1) // width
        for r in range(r_count):
            full = dot(ops[r * d : (r + 1) * d, :], spread)
            bd_out[r * d : (r + 1) * d, :] = jnp.where(inside, full, 0.0).astype(BF16)
        neg_hot = hot_rows(column(negs[...]), table.shape[0])
        neg_rows[...] = dot(neg_hot, table[...]).astype(BF16)
        neg_acc[...] = jnp.zeros_like(neg_acc)

    head_wide = dot(hot_rows(column(heads[0]), table.shape[0]), table[...])
    head = head_wide.astype(BF16)
    turned_out[...] = head_wide.T.astype(BF16)
    rel_col = column(rels[0])
    proj = jnp.zeros((TILE, d), F32)
    for r in range(r_count):
        masked = jnp.where(rel_col == r, head_wide, 0.0).astype(BF16)
        proj = proj + dot(masked, bd_out[r * d : (r + 1) * d, :])
    proj = proj.astype(BF16)
    proj_out[...] = proj
    negative = lax.dot_general(proj, neg_rows[...], CONTRACT_LAST, preferred_element_type=F32)
    live = step * TILE + iota((TILE, n_neg), 0) < scal[1]
    weight = jnp.where(live, jax.nn.sigmoid(negative) / n_neg, 0.0)
    negpart_out[...] = dot(weight.astype(BF16), neg_rows[...])
    neg_acc[...] += dot(weight.T.astype(BF16), proj)

    @pl.when(step == pl.num_programs(0) - 1)
    def _():
        grads = neg_acc[...].astype(BF16)
        for k in range(table.shape[0] // TILE):
            hot = hot_columns(negs[...] - k * TILE, TILE)
            nege_out[k * TILE : (k + 1) * TILE, :] = dot(hot, grads)


def tail_kernel(n_rel, share, scal, tails, proj, negpart, *refs):
    chunks, (gp_out, *outs), (weighted, places) = (
        refs[:n_rel], refs[n_rel : 2 * n_rel + 1], refs[2 * n_rel + 1 :],
    )
    step = pl.program_id(0)
    rows = chunks[0].shape[0]
    slots = share * n_rel
    t = tails[0]
    slot = t % slots
    place = (slot // share - scal[0] + n_rel) % n_rel * rows
    place = place + t // slots * share + slot % share
    places[:, pl.ds(pl.multiple_of(step * TILE, TILE), TILE)] = place
    col = column(place)
    tail = jnp.zeros((TILE, proj.shape[1]), F32)
    for c in range(n_rel):
        tail = tail + dot(hot_rows(col - c * rows, rows), chunks[c][...])
    wide = proj[...].astype(F32)
    positive = jnp.sum(wide * tail, axis=1, keepdims=True)
    live = step * TILE + iota((TILE, 1), 0) < scal[1]
    pos_weight = jnp.where(live, -jax.nn.sigmoid(-positive), 0.0)
    gp_out[...] = (pos_weight * tail + negpart[...]).astype(BF16)
    weighted[pl.ds(pl.multiple_of(step * TILE, TILE), TILE), :] = (pos_weight * wide).astype(BF16)

    @pl.when(step == pl.num_programs(0) - 1)
    def _():
        for c in range(n_rel):
            hot = hot_columns(places[...] - c * rows, rows)
            outs[c][...] = dot(hot, weighted[...]).astype(BF16)


def grad_kernel(
    blocks, heads, rels, gp, turned, nege, bd,
    rel_out, rows_out, head_acc,
):
    step = pl.program_id(0)
    edges, d = gp.shape
    width = d // blocks
    rel_row = rels[...]
    grads = gp[...]

    @pl.when(step == 0)
    def _():
        head_acc[...] = jnp.zeros_like(head_acc)

    masked = jnp.where(rel_row == step, turned[...].astype(F32), 0.0).astype(BF16)
    outer = dot(masked, grads)
    inside = iota((d, d), 0) // width == iota((d, d), 1) // width
    outer = jnp.where(inside, outer, 0.0)
    packed = outer[:width]
    for n in range(1, blocks):
        packed = packed + outer[n * width : (n + 1) * width]
    for half in range(d // 128):
        start = pl.multiple_of((half * pl.num_programs(0) + step) * width, width)
        rel_out[pl.ds(start, width), :] = packed[:, half * 128 : (half + 1) * 128].astype(BF16)
    for k in range(edges // TILE):
        part = pl.ds(k * TILE, TILE)
        rel_col = column(rel_row[:, k * TILE : (k + 1) * TILE])
        mine = jnp.where(rel_col == step, gp[part, :].astype(F32), 0.0).astype(BF16)
        head_acc[part, :] += lax.dot_general(mine, bd[...], CONTRACT_LAST, preferred_element_type=F32)

    @pl.when(step == pl.num_programs(0) - 1)
    def _():
        head_grad = head_acc[...].astype(BF16)
        for k in range(nege.shape[0] // TILE):
            part = slice(k * TILE, (k + 1) * TILE)
            rows_out[part, :] = nege[part, :] + dot(hot_columns(heads[...] - k * TILE, TILE), head_grad)


def owner_kernel(n_rel, scal, ids, returned, terms, *outs):
    d = terms.shape[1]
    rows = terms.shape[0] // n_rel
    for c in range(n_rel):
        start = pl.multiple_of((scal[0] + c) % n_rel * rows, rows)
        total = terms[pl.ds(start, rows), :]
        total = total + dot(hot_columns(ids[...] - start, rows), returned[:, :d])
        outs[c][...] = total.astype(BF16)


def place_kernel(n_rel, scal, *refs):
    out = refs[n_rel]
    rows = out.shape[0] // n_rel
    for c in range(n_rel):
        start = pl.multiple_of((scal[0] + c) % n_rel * rows, rows)
        out[pl.ds(start, rows), :] = refs[c][...].astype(F32)


def relation_kernel(r_count, blocks, width, x, out):
    per = 128 // width
    for r in range(r_count):
        for n in range(blocks):
            start = (n // per * r_count + r) * width
            block = x[start : start + width, n % per * width : (n % per + 1) * width]
            out[r, n] = block.astype(F32)


def ring(x, n_rel, shift):
    return lax.ppermute(x, "rel", [((k + shift) % n_rel, k) for k in range(n_rel)])


def local(
    entity_rows, request_rows, edge_heads, edge_rels, edge_tails, edge_counts, negative_rows,
    relation_blocks,
):
    rows, d = entity_rows.shape
    parts, slots = request_rows.shape[1:]
    r_count, blocks, width = relation_blocks.shape[:3]
    edges, n_neg = edge_heads.shape[0], negative_rows.shape[0]
    n_rel = lax.axis_size("rel")
    share = slots // n_rel
    held = parts * share
    steps = edges // TILE
    me = lax.axis_index("rel").astype(jnp.int32)
    scal = jnp.concatenate([me.reshape(1), edge_counts])
    shaped = jax.ShapeDtypeStruct

    lists = lax.all_to_all(request_rows.reshape(parts, 1, slots), "ent", 0, 0, tiled=True)
    lists = lists.reshape(parts, slots)

    heads = edge_heads.reshape(steps, 1, TILE)
    rels = edge_rels.reshape(steps, 1, TILE)
    tails = edge_tails.reshape(steps, 1, TILE)
    negs = negative_rows.reshape(1, n_neg)
    id_block = pl.BlockSpec((1, 1, TILE), lambda i: (i, 0, 0))
    edge_block = pl.BlockSpec((TILE, d), lambda i: (i, 0))

    table = pl.pallas_call(
        stage_kernel,
        in_specs=[whole((rows, d))],
        out_specs=whole((rows, d)),
        out_shape=shaped((rows, d), BF16),
        compiler_params=params(0),
        cost_estimate=cost(1e6, 1e6),
        name="stage",
    )(entity_rows)
    picked = pl.pallas_call(
        functools.partial(pick_kernel, share),
        in_specs=[SMEM, whole((parts, slots)), whole((rows, d))],
        out_specs=whole((held, d)),
        out_shape=shaped((held, d), BF16),
        compiler_params=params(0),
        cost_estimate=cost(2 * held * rows * d, 1e6),
        name="pick",
    )(scal, lists, table)
    proj, negpart, turned, nege, bd = pl.pallas_call(
        functools.partial(head_kernel, r_count, blocks),
        grid=(steps,),
        in_specs=[
            SMEM, id_block, id_block, whole((1, n_neg)), whole((rows, d)),
            whole((r_count * d, width)),
        ],
        out_specs=[
            edge_block, edge_block, pl.BlockSpec((d, TILE), lambda i: (0, i)), whole((rows, d)),
            whole((r_count * d, d)),
        ],
        out_shape=[
            shaped((edges, d), BF16), shaped((edges, d), F32), shaped((d, edges), BF16),
            shaped((rows, d), F32), shaped((r_count * d, d), BF16),
        ],
        scratch_shapes=[pltpu.VMEM((n_neg, d), BF16), pltpu.VMEM((n_neg, d), F32)],
        compiler_params=params(),
        cost_estimate=cost(3e9, 6e6),
        name="head_step",
    )(scal, heads, rels, negs, entity_rows, relation_blocks.reshape(r_count * d, width))

    fetched = lax.all_to_all(picked, "ent", 0, 0, tiled=True)
    fetched = [fetched] + [ring(fetched, n_rel, c) for c in range(1, n_rel)]

    grad_proj, *slot_parts = pl.pallas_call(
        functools.partial(tail_kernel, n_rel, share),
        grid=(steps,),
        in_specs=[SMEM, id_block, edge_block, edge_block, ] + [whole((held, d))] * n_rel,
        out_specs=[edge_block] + [whole((held, d))] * n_rel,
        out_shape=[shaped((edges, d), BF16)] + [shaped((held, d), BF16)] * n_rel,
        scratch_shapes=[pltpu.VMEM((edges, d), BF16), pltpu.VMEM((1, edges), jnp.int32)],
        compiler_params=params(),
        cost_estimate=cost(3e9, 5e6),
        name="tail_step",
    )(scal, tails, proj, negpart, *fetched)
    list_rows = pl.pallas_call(
        functools.partial(rows_kernel, share),
        in_specs=[SMEM, whole((parts, slots)), ANY],
        out_specs=whole((1, held)),
        out_shape=shaped((1, held), jnp.int32),
        compiler_params=params(0),
        cost_estimate=cost(1e8, 1e5),
        name="list_rows",
    )(scal, lists, grad_proj)
    slot_sum = slot_parts[0].astype(F32)
    for c in range(1, n_rel):
        slot_sum = slot_sum + ring(slot_parts[c], n_rel, n_rel - c).astype(F32)

    rel_part, row_terms = pl.pallas_call(
        functools.partial(grad_kernel, blocks),
        grid=(r_count,),
        in_specs=[
            whole((1, edges)), whole((1, edges)), whole((edges, d)), whole((d, edges)),
            whole((rows, d)), pl.BlockSpec((d, d), lambda r: (r, 0)),
        ],
        out_specs=[whole((r_count * width * d // 128, 128)), whole((rows, d))],
        out_shape=[shaped((r_count * width * d // 128, 128), BF16), shaped((rows, d), F32)],
        scratch_shapes=[pltpu.VMEM((edges, d), F32)],
        compiler_params=params(),
        cost_estimate=cost(3e9, 6e6),
        name="grad_step",
    )(edge_heads.reshape(1, edges), edge_rels.reshape(1, edges), grad_proj, turned, nege, bd)

    packed = jnp.concatenate([slot_sum.astype(BF16), rel_part], axis=1)
    returned = lax.all_to_all(packed, "ent", 0, 0, tiled=True)
    rel_sum = jnp.sum(returned[:, d:].reshape(parts, -1, 128).astype(F32), 0).astype(BF16)
    rel_all = jnp.broadcast_to(rel_sum[None], (parts,) + rel_sum.shape).reshape(-1, 128)
    rel_all = lax.all_to_all(rel_all, "ent", 0, 0, tiled=True)

    row_parts = pl.pallas_call(
        functools.partial(owner_kernel, n_rel),
        in_specs=[SMEM, whole((1, held)), whole(returned.shape), whole((rows, d))],
        out_specs=[whole((rows // n_rel, d))] * n_rel,
        out_shape=[shaped((rows // n_rel, d), BF16)] * n_rel,
        compiler_params=params(0),
        cost_estimate=cost(3e8, 2e6),
        name="owner_add",
    )(scal, list_rows, returned, row_terms)
    row_sum = row_parts[0].astype(F32)
    for c in range(1, n_rel):
        row_sum = row_sum + ring(row_parts[c], n_rel, n_rel - c).astype(F32)
    row_sum = row_sum.astype(BF16)
    row_sums = [row_sum] + [ring(row_sum, n_rel, c) for c in range(1, n_rel)]
    entity_grad = pl.pallas_call(
        functools.partial(place_kernel, n_rel),
        in_specs=[SMEM] + [whole((rows // n_rel, d))] * n_rel,
        out_specs=whole((rows, d)),
        out_shape=shaped((rows, d), F32),
        compiler_params=params(0),
        cost_estimate=cost(1e6, 1.5e6),
        name="place_rows",
    )(scal, *row_sums)
    rel_all, entity_grad = lax.optimization_barrier((rel_all, entity_grad))
    relation_grad = pl.pallas_call(
        functools.partial(relation_kernel, r_count, blocks, width),
        in_specs=[whole(rel_all.shape)],
        out_specs=whole(relation_blocks.shape),
        out_shape=shaped(relation_blocks.shape, F32),
        compiler_params=params(0),
        cost_estimate=cost(1e6, 1.2e6),
        name="relation_out",
    )(rel_all)
    return entity_grad, relation_grad


def solution(mesh):
    in_specs = (
        P("ent", None),
        P("ent", None, None),
        P(("ent", "rel")),
        P(("ent", "rel")),
        P(("ent", "rel")),
        P(("ent", "rel")),
        P(("ent", "rel")),
        P("rel", None, None, None),
    )
    out_specs = (P("ent", None), P("rel", None, None, None))
    return jax.shard_map(local, mesh=mesh, in_specs=in_specs, out_specs=out_specs, check_vma=False)
```
